32 devices in a mesh: dp: 16 (over z, y, x), mp: 2 (over core).
Axes of the slice: x: 2, y: 2, z: 4, core: 2. Of those that a mesh axis runs over, the one named last changes fastest.
Arguments:
- clean_latent: float32 [16, 4096], P('dp'), may hold values from -6 to 6
- noise_draw: float32 [16, 4096], P('dp'), may hold values from -6 to 6
- timestep: int32 [16], P('dp'), may hold values from 1 to 8
- bucket: int32 [16], P('dp'), may hold values from 0 to 7
- bucket_weights: float32 [8], replicated, may hold values from 0.25 to 4
- teacher_embed: float32 [16, 2048], replicated, may hold values from -1.5 to 1.5
- teacher_final: float32 [16, 2048], replicated, may hold values from -0.125 to 0.125
- teacher_mod: float32 [16, 3, 2048], replicated, may hold values from -3 to 3
- teacher_qkv: bfloat16 [2048, 3, 1024], P(None, None, 'mp'), may hold values from -1 to 1
- teacher_out: bfloat16 [2048, 1024], P(None, 'mp'), may hold values from -0.1875 to 0.1875
- student_embed: float32 [16, 2048], replicated, may hold values from -1.5 to 1.5
- student_final: float32 [16, 2048], replicated, may hold values from -0.125 to 0.125
- student_mod: float32 [8, 3, 2048], replicated, may hold values from -3 to 3
- student_qkv: bfloat16 [2048, 3, 1024], P('dp', None, 'mp'), may hold values from -1 to 1
- student_out: bfloat16 [2048, 1024], P('dp', 'mp'), may hold values from -0.1875 to 0.1875
- moment_qkv: float32 [2048, 3, 1024], P('dp', None, 'mp'), may hold values from -2 to 2
- second_qkv: float32 [2048, 3, 1024], P('dp', None, 'mp'), may hold values from 0.05 to 0.5
- moment_out: float32 [2048, 1024], P('dp', 'mp'), may hold values from -2 to 2
- second_out: float32 [2048, 1024], P('dp', 'mp'), may hold values from 0.05 to 0.5
Outputs:
- new_moment_qkv: float32 [2048, 3, 1024], P('dp', None, 'mp')
- new_second_qkv: float32 [2048, 3, 1024], P('dp', None, 'mp')
- update_qkv: float32 [2048, 3, 1024], P('dp', None, 'mp')
- new_moment_out: float32 [2048, 1024], P('dp', 'mp')
- new_second_out: float32 [2048, 1024], P('dp', 'mp')
- update_out: float32 [2048, 1024], P('dp', 'mp')
- loss: float32 [], replicated
The draws below stay inside these ranges and needn't reach their ends.
All inputs are finite; a program needn't handle non-finite values.
Results may differ from the reference program's by a relative error of at most 0.00035.
Values may be sent and summed in bfloat16 or wider, within the bound.
A program may use at most 128 MiB of HBM per device.

```python
import math
import jax
import jax.numpy as jnp
from jax import lax

D = 2048
HEADS = 16
HS = 64
INNER = 1024
PATCH_CH = 16
SEQ = 256
LATENT = 4096
SAMPLES = 16
K = 8
TGRID = 16
NBUCKET = 8


def aligned_projection(seed_key, salt):
    folded = jax.random.fold_in(seed_key, salt)
    initial = jax.random.normal(folded, (D, 3, INNER), jnp.float32) / math.sqrt(D)
    return jnp.clip(initial, -1.0, 1.0).astype(jnp.bfloat16)


def draw_teacher_qkv(key, part):
    return aligned_projection(key, 11)


def draw_student_qkv(key, part):
    return aligned_projection(key, 23)


def set_ends(entries, key, smallest, largest):
    place = [jax.random.randint(jax.random.fold_in(key, axis), (), 0, length) for axis, length in enumerate(entries.shape)]
    longest = entries.shape.index(max(entries.shape))
    next_to = place[:longest] + [(place[longest] + 1) % entries.shape[longest]] + place[longest + 1:]
    return entries.at[tuple(place)].set(smallest).at[tuple(next_to)].set(largest)


def block_scale(key, extent, shards, least, high):
    gain = 1.0
    for position, blocks in shards:
        draws = jax.random.uniform(jax.random.fold_in(jax.random.fold_in(key, 6), position), (blocks,), jnp.float32, least / len(shards), high / len(shards))
        gain = gain * jnp.repeat(jnp.exp(draws), extent[position] // blocks).reshape((-1,) + (1,) * (len(extent) - 1 - position))
    return gain


def noise(rng, extent, scale, bound, shards=(), kind=jnp.bfloat16):
    values = jax.random.normal(rng, extent, jnp.float32) * scale
    if len(shards) > 0:
        values = block_scale(rng, extent, shards, -0.22, 0.18) * values
    return jnp.clip(values, min=-bound, max=bound).astype(kind)


def setup_inputs(seed: int = 0) -> dict:
    splits = jax.random.split(jax.random.key(seed), 20)
    return {
        "clean_latent": noise(splits[0], (SAMPLES, LATENT), 1.0, 6.0, ((0, 16),), jnp.float32),
        "noise_draw": noise(splits[1], (SAMPLES, LATENT), 1.0, 6.0, ((0, 16),), jnp.float32),
        "timestep": set_ends(jax.random.randint(splits[2], (SAMPLES,), 1, K + 1), jax.random.fold_in(splits[2], 1), 1, K).astype(jnp.int32),
        "bucket": set_ends(jax.random.randint(splits[3], (SAMPLES,), 0, NBUCKET), jax.random.fold_in(splits[3], 1), 0, NBUCKET - 1).astype(jnp.int32),
        "bucket_weights": jnp.clip(jnp.exp(jax.random.uniform(splits[4], (NBUCKET,), jnp.float32, math.log(0.25), math.log(4.0))), 0.25, 4.0),
        "teacher_embed": noise(splits[5], (PATCH_CH, D), PATCH_CH ** -0.5, 1.5, (), jnp.float32),
        "teacher_final": noise(splits[6], (PATCH_CH, D), D ** -0.5, 0.125, (), jnp.float32),
        "teacher_mod": noise(splits[7], (TGRID, 3, D), 0.5, 3.0, (), jnp.float32),
        "teacher_qkv": draw_teacher_qkv(jax.random.fold_in(splits[19], 71), 0),
        "teacher_out": noise(splits[9], (D, INNER), INNER ** -0.5, 0.1875, ((1, 2),)),
        "student_embed": noise(splits[10], (PATCH_CH, D), PATCH_CH ** -0.5, 1.5, (), jnp.float32),
        "student_final": noise(splits[11], (PATCH_CH, D), D ** -0.5, 0.125, (), jnp.float32),
        "student_mod": noise(splits[12], (K, 3, D), 0.5, 3.0, (), jnp.float32),
        "student_qkv": draw_student_qkv(jax.random.fold_in(splits[19], 71), 0),
        "student_out": noise(splits[14], (D, INNER), INNER ** -0.5, 0.1875, ((0, 16), (1, 2))),
        "moment_qkv": noise(splits[15], (D, 3, INNER), 0.3, 2.0, ((0, 16), (2, 2)), jnp.float32),
        "second_qkv": jnp.clip(jnp.exp(math.log(0.5) - 2.3025851 * jax.random.uniform(splits[16], (D, 3, INNER), jnp.float32) ** block_scale(splits[16], (D, 3, INNER), ((0, 16), (2, 2)), -0.2, 0.2)), 0.05, 0.5),
        "moment_out": noise(splits[17], (D, INNER), 0.3, 2.0, ((0, 16), (1, 2)), jnp.float32),
        "second_out": jnp.clip(jnp.exp(math.log(0.5) - 2.3025851 * jax.random.uniform(splits[18], (D, INNER), jnp.float32) ** block_scale(splits[18], (D, INNER), ((0, 16), (1, 2)), -0.2, 0.2)), 0.05, 0.5),
    }


LN_EPS = 0.01
BETA_ONE = 0.9
BETA_TWO = 0.99
ADAM_EPS = 1e-08

def plan():
    grid = jnp.arange(TGRID + 1, dtype=jnp.float32)
    lamb = 6.0 - 12.0 * grid / TGRID
    return (jnp.sqrt(jax.nn.sigmoid(lamb)), jnp.sqrt(jax.nn.sigmoid(-lamb)))

def positions():
    index = jnp.arange(SEQ, dtype=jnp.float32)[:, None]
    half = D // 2
    freqs = jnp.exp(-math.log(10000.0) * jnp.arange(half, dtype=jnp.float32) / half)
    angles = index * freqs[None, :]
    return jnp.concatenate([jnp.sin(angles), jnp.cos(angles)], axis=1)

def normalize(values):
    center = values - lax.optimization_barrier(jnp.mean(values, axis=-1, keepdims=True))
    inverse = lax.rsqrt(lax.optimization_barrier(jnp.mean(center * center, axis=-1, keepdims=True)) + LN_EPS)
    return (center * inverse, inverse)

def norm_back(upstream, normed, inverse):
    first_mean = lax.optimization_barrier(jnp.mean(upstream, axis=-1, keepdims=True))
    second_mean = lax.optimization_barrier(jnp.mean(upstream * normed, axis=-1, keepdims=True))
    return (upstream - first_mean - normed * second_mean) * inverse

def front(latent, modrow, embed, w_qkv, w_out, placed):
    hidden = jnp.dot(latent, embed, precision=lax.Precision.HIGHEST) + placed
    normed, unused = normalize(hidden)
    shaped = (normed * (1.0 + modrow[1]) + modrow[0]).astype(jnp.bfloat16)
    packed = jnp.dot(shaped, w_qkv.reshape(D, 3 * INNER), preferred_element_type=jnp.float32)
    packed = packed.astype(jnp.bfloat16).reshape(SEQ, 3, HEADS, HS)
    queries = packed[:, 0]
    keys_all = packed[:, 1]
    values = packed[:, 2]
    scores = jnp.einsum('qhd,khd->hqk', queries.astype(jnp.float32), keys_all.astype(jnp.float32)) / math.sqrt(HS)
    weights = jax.nn.softmax(scores, axis=-1)
    rounded = weights.astype(jnp.bfloat16)
    attended = jnp.einsum('hqk,khd->qhd', rounded.astype(jnp.float32), values.astype(jnp.float32))
    attended = attended.astype(jnp.bfloat16).reshape(SEQ, INNER)
    projected = lax.dot_general(attended, w_out, (((1,), (1,)), ((), ())), preferred_element_type=jnp.float32)
    return (hidden, shaped, queries, keys_all, values, weights, rounded, attended, projected)

def tail(hidden, modrow, projected, final):
    mixed = hidden + modrow[2] * projected
    normed, inverse = normalize(mixed)
    predicted = jnp.dot(normed, final.T, precision=lax.Precision.HIGHEST)
    return (predicted, normed, inverse)

def reference(clean_latent, noise_draw, timestep, bucket, bucket_weights, teacher_embed, teacher_final, teacher_mod, teacher_qkv, teacher_out, student_embed, student_final, student_mod, student_qkv, student_out, moment_qkv, second_qkv, moment_out, second_out):
    alphas, sigmas = plan()
    placed = positions()

    def teacher_eps(latent, modrow):
        parts = front(latent, modrow, teacher_embed, teacher_qkv, teacher_out, placed)
        return tail(parts[0], modrow, parts[8], teacher_final)[0]

    def sample_step(carry, inputs):
        clean_row, noise_row, step_index, bucket_id = inputs
        first = 2 * step_index
        middle = first - 1
        last = first - 2
        a_first, s_first = (alphas[first], sigmas[first])
        a_middle, s_middle = (alphas[middle], sigmas[middle])
        a_last, s_last = (alphas[last], sigmas[last])
        latent0 = (a_first * clean_row + s_first * noise_row).reshape(SEQ, PATCH_CH)
        eps_zero = teacher_eps(latent0, teacher_mod[first - 1])
        latent1 = a_middle * (latent0 - s_first * eps_zero) / a_first + s_middle * eps_zero
        eps_one = teacher_eps(latent1, teacher_mod[middle - 1])
        latent2 = a_last * (latent1 - s_middle * eps_one) / a_middle + s_last * eps_one
        target = (latent0 - a_first / a_last * latent2) / (s_first - a_first * s_last / a_last)
        modrow = student_mod[step_index - 1]
        hidden, shaped, queries, keys_all, values, weights, rounded, attended, projected = front(latent0, modrow, student_embed, student_qkv, student_out, placed)
        predicted, normed, inverse = tail(hidden, modrow, projected, student_final)
        weight = bucket_weights[bucket_id]
        error = predicted - target
        sample_loss = weight * jnp.sum(error * error)
        d_pred = 2.0 * weight * error
        d_normed = jnp.dot(d_pred, student_final, precision=lax.Precision.HIGHEST)
        d_mixed = norm_back(d_normed, normed, inverse)
        d_proj = (modrow[2] * d_mixed).astype(jnp.bfloat16)
        grad_out = lax.dot_general(d_proj, attended, (((0,), (0,)), ((), ())), preferred_element_type=jnp.float32)
        d_attn = jnp.dot(d_proj, student_out, preferred_element_type=jnp.float32).astype(jnp.bfloat16)
        d_attn = d_attn.reshape(SEQ, HEADS, HS).astype(jnp.float32)
        d_prob = jnp.einsum('qhd,khd->hqk', d_attn, values.astype(jnp.float32))
        d_score = (weights * (d_prob - lax.optimization_barrier(jnp.sum(weights * d_prob, axis=-1, keepdims=True))) / math.sqrt(HS)).astype(jnp.bfloat16)
        d_score = d_score.astype(jnp.float32)
        d_query = jnp.einsum('hqk,khd->qhd', d_score, keys_all.astype(jnp.float32)).astype(jnp.bfloat16)
        d_key = jnp.einsum('hqk,qhd->khd', d_score, queries.astype(jnp.float32)).astype(jnp.bfloat16)
        d_value = jnp.einsum('hqk,qhd->khd', rounded.astype(jnp.float32), d_attn).astype(jnp.bfloat16)
        d_pack = jnp.stack([d_query, d_key, d_value], axis=1).reshape(SEQ, 3 * INNER)
        grad_qkv = lax.dot_general(shaped, d_pack, (((0,), (0,)), ((), ())), preferred_element_type=jnp.float32)
        return ((carry[0] + grad_qkv, carry[1] + grad_out, carry[2] + sample_loss), None)
    start_carry = (jnp.zeros((D, 3 * INNER), jnp.float32), jnp.zeros((D, INNER), jnp.float32), jnp.zeros((), jnp.float32))
    sums, unused = lax.scan(sample_step, start_carry, (clean_latent, noise_draw, timestep, bucket))
    grad_qkv = sums[0].reshape(D, 3, INNER)
    grad_out = sums[1]
    squares = jnp.sum(grad_qkv * grad_qkv) + jnp.sum(grad_out * grad_out)
    rms_value = jnp.sqrt(squares / (4 * D * INNER))
    factor = 1.0 / jnp.maximum(rms_value, 1.0)

    def adam(moment, second, grad):
        normed_grad = grad * factor
        new_moment = BETA_ONE * moment + (1.0 - BETA_ONE) * normed_grad
        new_second = BETA_TWO * second + (1.0 - BETA_TWO) * normed_grad * normed_grad
        return (new_moment, new_second, new_moment / (jnp.sqrt(new_second) + ADAM_EPS))
    mq, vq, uq = adam(moment_qkv, second_qkv, grad_qkv)
    mo, vo, uo = adam(moment_out, second_out, grad_out)
    loss = sums[2] / (SAMPLES * LATENT)
    return (mq, vq, uq, mo, vo, uo, loss)
```

```python
import functools
import math

import jax
import jax.numpy as jnp
from jax import lax
from jax.experimental import pallas as pl
from jax.experimental.pallas import tpu as pltpu
from jax.sharding import PartitionSpec as P

D = 2048
HS = 64
INNER = 1024
PATCH_CH = 16
SEQ = 256
LATENT = 4096
K = 8
TGRID = 16
NBUCKET = 8


LN_EPS = 0.01
BETA_ONE = 0.9
BETA_TWO = 0.99
ADAM_EPS = 1e-08


def plan():
    grid = jnp.arange(TGRID + 1, dtype=jnp.float32)
    lamb = 6.0 - 12.0 * grid / TGRID
    return (jnp.sqrt(jax.nn.sigmoid(lamb)), jnp.sqrt(jax.nn.sigmoid(-lamb)))


def positions():
    index = jnp.arange(SEQ, dtype=jnp.float32)[:, None]
    half = D // 2
    freqs = jnp.exp(-math.log(10000.0) * jnp.arange(half, dtype=jnp.float32) / half)
    angles = index * freqs[None, :]
    return jnp.concatenate([jnp.sin(angles), jnp.cos(angles)], axis=1)


def normalize(values):
    center = values - jnp.mean(values, axis=-1, keepdims=True)
    inverse = lax.rsqrt(jnp.mean(center * center, axis=-1, keepdims=True) + LN_EPS)
    return (center * inverse, inverse)


def norm_back(upstream, normed, inverse):
    first_mean = jnp.mean(upstream, axis=-1, keepdims=True)
    second_mean = jnp.mean(upstream * normed, axis=-1, keepdims=True)
    return (upstream - first_mean - normed * second_mean) * inverse


def one_hot_rows(index, width):
    return (index[:, None] == jnp.arange(width, dtype=jnp.int32)[None, :]).astype(jnp.float32)


USE_KERNEL = True


def exchange_kernel(size, blocks, x_ref, out_ref, send_sem, recv_sem, own_sem):
    me = lax.axis_index("dp")
    base = (me // size) * size
    pos = me - base
    rows = out_ref.shape[0] // size

    def peer_of(step):
        if size & (size - 1):
            return lax.rem(pos + step, size)
        peer = pos
        bit = 1
        while bit < size:
            if step & bit:
                peer = peer + bit * (1 - 2 * ((pos // bit) % 2))
            bit *= 2
        return peer

    def source(member):
        start = lax.rem(member, blocks) * rows
        return x_ref.at[pl.ds(pl.multiple_of(start, rows), rows)]

    mine = out_ref.at[pl.ds(pl.multiple_of(pos * rows, rows), rows)]
    barrier = pltpu.get_barrier_semaphore()
    for step in range(1, size):
        pl.semaphore_signal(
            barrier,
            inc=1,
            device_id={"dp": base + peer_of(step)},
            device_id_type=pl.DeviceIdType.MESH,
        )
    pl.semaphore_wait(barrier, size - 1)
    copies = []
    for step in range(1, size):
        peer = peer_of(step)
        copy = pltpu.make_async_remote_copy(
            src_ref=source(peer),
            dst_ref=mine,
            send_sem=send_sem.at[step],
            recv_sem=recv_sem.at[step],
            device_id={"dp": base + peer},
            device_id_type=pl.DeviceIdType.MESH,
        )
        copy.start()
        copies.append(copy)
    own = pltpu.make_async_copy(source(pos), mine, own_sem)
    own.start()
    own.wait()
    for copy in copies:
        copy.wait()


def exchange(x, size, blocks, ident):
    rows = x.shape[0] // blocks
    if not USE_KERNEL:
        total = lax.axis_size("dp")
        groups = None
        if size != total:
            groups = [list(range(b, b + size)) for b in range(0, total, size)]
        wide = jnp.tile(x, (size // blocks, 1))
        return lax.all_to_all(wide, "dp", 0, 0, axis_index_groups=groups, tiled=True)
    return pl.pallas_call(
        functools.partial(exchange_kernel, size, blocks),
        out_shape=jax.ShapeDtypeStruct((size * rows, x.shape[1]), x.dtype),
        in_specs=[pl.BlockSpec(memory_space=pl.ANY)],
        out_specs=pl.BlockSpec(memory_space=pl.ANY),
        scratch_shapes=[
            pltpu.SemaphoreType.DMA((size,)),
            pltpu.SemaphoreType.DMA((size,)),
            pltpu.SemaphoreType.DMA,
        ],
        compiler_params=pltpu.CompilerParams(collective_id=ident, has_side_effects=True),
        cost_estimate=pl.CostEstimate(
            flops=0, bytes_accessed=16 * size * rows * x.shape[1], transcendentals=0
        ),
    )(x)


def per_device(
    clean_latent,
    noise_draw,
    timestep,
    bucket,
    bucket_weights,
    teacher_embed,
    teacher_final,
    teacher_mod,
    teacher_qkv,
    teacher_out,
    student_embed,
    student_final,
    student_mod,
    student_qkv,
    student_out,
    moment_qkv,
    second_qkv,
    moment_out,
    second_out,
):
    samples = clean_latent.shape[0]
    rows_all = samples * SEQ
    local_inner = teacher_out.shape[1]
    local_heads = local_inner // HS
    devices = lax.axis_size("dp")
    members = local_heads
    pictures = members * samples
    group_rows = pictures * SEQ
    own_rows = D // devices
    halves = lax.axis_size("mp")
    count = rows_all // halves
    half = lax.axis_index("mp")
    start = half * count
    swap = [(0, 1), (1, 0)]

    def take(values):
        return lax.dynamic_slice_in_dim(values, start, count, 0)

    alphas, sigmas = plan()
    table = jnp.stack([alphas, sigmas], axis=1)

    def coefficients(tau):
        picked = jnp.dot(one_hot_rows(tau, TGRID + 1), table, precision=lax.Precision.HIGHEST)
        picked = jnp.repeat(picked, SEQ, axis=0)
        return (picked[:, 0:1], picked[:, 1:2])

    def modulation(mod_table, index):
        return jnp.take(mod_table, index, axis=0, mode="clip")

    def gate_rows(modrows):
        return take(jnp.repeat(modrows[:, 2], SEQ, axis=0))

    placed = positions()

    def shape_rows(latent, modrows, embed, pictured):
        hidden = (
            jnp.dot(latent, embed, precision=lax.Precision.HIGHEST).reshape(pictured, SEQ, D)
            + placed[None]
        )
        normed, unused = normalize(hidden)
        shaped = (
            (normed * (1.0 + modrows[:, None, 1]) + modrows[:, None, 0])
            .astype(jnp.bfloat16)
            .reshape(pictured * SEQ, D)
        )
        return (hidden.reshape(pictured * SEQ, D), shaped)

    def attend(queries, keys_all, values):
        scores = jnp.einsum(
            "bqd,bkd->bqk", queries, keys_all, preferred_element_type=jnp.float32
        ) / math.sqrt(HS)
        highest = jnp.max(scores, axis=-1, keepdims=True)
        expos = jnp.exp(scores - highest)
        weights = expos / jnp.sum(expos, axis=-1, keepdims=True)
        rounded = weights.astype(jnp.bfloat16)
        attended = jnp.einsum(
            "bqk,bkd->bqd", rounded, values, preferred_element_type=jnp.float32
        ).astype(jnp.bfloat16)
        return (weights, rounded, attended)

    def project(attended, w_out):
        return lax.dot_general(
            attended, w_out, (((1,), (1,)), ((), ())), preferred_element_type=jnp.float32
        )

    def reduce_heads(projected):
        if halves != 2:
            return lax.psum_scatter(projected, "mp", scatter_dimension=0, tiled=True)
        away = lax.dynamic_slice_in_dim(projected, count - start, count, 0)
        return take(projected) + lax.ppermute(away, "mp", swap)

    def join_halves(mine):
        if halves != 2:
            return lax.all_gather(mine, "mp", axis=0, tiled=True)
        other = lax.ppermute(mine, "mp", swap)
        first_half = jnp.where(half == 0, mine, other)
        second_half = jnp.where(half == 0, other, mine)
        return jnp.concatenate([first_half, second_half], axis=0)

    def tail(hidden_mine, modrows, projected, final):
        mixed = hidden_mine + gate_rows(modrows) * reduce_heads(projected)
        normed, inverse = normalize(mixed)
        predicted = lax.dot_general(
            normed, final, (((1,), (1,)), ((), ())), precision=lax.Precision.HIGHEST
        )
        return (predicted, normed, inverse)

    def teacher_eps(latent, modrows):
        hidden, shaped = shape_rows(latent, modrows, teacher_embed, samples)
        packed = jnp.dot(
            shaped, teacher_qkv.reshape(D, 3 * local_inner), preferred_element_type=jnp.float32
        )
        packed = packed.astype(jnp.bfloat16).reshape(samples, SEQ, 3, local_heads, HS)
        packed = packed.transpose(2, 0, 3, 1, 4).reshape(3, samples * local_heads, SEQ, HS)
        attended = attend(packed[0], packed[1], packed[2])[2]
        attended = attended.reshape(samples, local_heads, SEQ, HS).transpose(0, 2, 1, 3)
        projected = project(attended.reshape(rows_all, local_inner), teacher_out)
        return tail(take(hidden), modrows, projected, teacher_final)[0]

    first = 2 * timestep
    middle = first - 1
    last = first - 2
    a_first, s_first = coefficients(first)
    a_middle, s_middle = coefficients(middle)
    a_last, s_last = coefficients(last)
    clean_rows = clean_latent.reshape(rows_all, PATCH_CH)
    noise_rows = noise_draw.reshape(rows_all, PATCH_CH)
    latent0 = a_first * clean_rows + s_first * noise_rows

    whole_out = lax.all_gather(student_out, "dp", axis=0, tiled=True)
    by_head = student_qkv.reshape(own_rows, 3, local_heads, HS).transpose(2, 0, 1, 3)
    head_qkv = exchange(by_head.reshape(local_heads * own_rows, 3 * HS), devices, local_heads, 0)
    lines = LATENT // 128
    stamped = jnp.concatenate(
        [
            latent0.reshape(samples, lines, 128),
            jnp.broadcast_to(timestep[:, None, None].astype(jnp.float32), (samples, 8, 128)),
        ],
        axis=1,
    )
    stamped = exchange(stamped.reshape(samples * (lines + 8), 128), members, 1, 5)
    stamped = stamped.reshape(pictures, lines + 8, 128)
    group_latent = stamped[:, :lines].reshape(group_rows, PATCH_CH)
    group_steps = stamped[:, lines, 0].astype(jnp.int32)
    unused, group_shaped = shape_rows(
        group_latent, modulation(student_mod, group_steps - 1), student_embed, pictures
    )
    packed = jnp.dot(group_shaped, head_qkv, preferred_element_type=jnp.float32)
    packed = packed.astype(jnp.bfloat16).reshape(pictures, SEQ, 3 * HS)
    queries = packed[:, :, :HS]
    keys_all = packed[:, :, HS : 2 * HS]
    values = packed[:, :, 2 * HS :]
    weights, rounded, attended = attend(queries, keys_all, values)
    attended = exchange(attended.reshape(group_rows, HS), members, members, 1)
    attended = attended.reshape(local_heads, rows_all, HS).transpose(1, 0, 2)
    attended = attended.reshape(rows_all, local_inner)
    attended_all = lax.all_gather(attended, "dp", axis=0, tiled=True)

    mine0 = take(latent0)
    af_mine, sf_mine = (take(a_first), take(s_first))
    am_mine, sm_mine = (take(a_middle), take(s_middle))
    al_mine, sl_mine = (take(a_last), take(s_last))
    eps_zero = teacher_eps(latent0, modulation(teacher_mod, first - 1))
    next_mine = am_mine * (mine0 - sf_mine * eps_zero) / af_mine + sm_mine * eps_zero
    latent1 = lax.all_gather(next_mine, "mp", axis=0, tiled=True)
    eps_one = teacher_eps(latent1, modulation(teacher_mod, middle - 1))
    latent2 = al_mine * (next_mine - sm_mine * eps_one) / am_mine + sl_mine * eps_one
    target = (mine0 - af_mine / al_mine * latent2) / (sf_mine - af_mine * sl_mine / al_mine)

    student_rows_mod = modulation(student_mod, timestep - 1)
    place_mine = take(jnp.tile(placed, (samples, 1)))
    hidden_mine = jnp.dot(mine0, student_embed, precision=lax.Precision.HIGHEST) + place_mine
    projected = project(attended, whole_out)
    predicted, normed, inverse = tail(hidden_mine, student_rows_mod, projected, student_final)
    sample_weight = jnp.dot(
        one_hot_rows(bucket, NBUCKET), bucket_weights, precision=lax.Precision.HIGHEST
    )
    row_weight = take(jnp.repeat(sample_weight, SEQ, axis=0)[:, None])
    error = predicted - target
    loss_part = jnp.sum(row_weight * error * error)
    d_pred = 2.0 * row_weight * error
    d_normed = jnp.dot(d_pred, student_final, precision=lax.Precision.HIGHEST)
    d_mixed = norm_back(d_normed, normed, inverse)
    d_proj_mine = (gate_rows(student_rows_mod) * d_mixed).astype(jnp.bfloat16)
    d_proj = join_halves(d_proj_mine)
    d_attn = jnp.dot(d_proj, whole_out, preferred_element_type=jnp.float32).astype(jnp.bfloat16)
    d_attn = d_attn.reshape(rows_all, local_heads, HS).transpose(1, 0, 2)
    d_attn = exchange(d_attn.reshape(local_heads * rows_all, HS), members, members, 2)
    d_attn = d_attn.reshape(pictures, SEQ, HS)
    d_prob = jnp.einsum("bqd,bkd->bqk", d_attn, values, preferred_element_type=jnp.float32)
    d_score = (
        weights * (d_prob - jnp.sum(weights * d_prob, axis=-1, keepdims=True)) / math.sqrt(HS)
    ).astype(jnp.bfloat16)
    d_query = jnp.einsum(
        "bqk,bkd->bqd", d_score, keys_all, preferred_element_type=jnp.float32
    ).astype(jnp.bfloat16)
    d_key = jnp.einsum(
        "bqk,bqd->bkd", d_score, queries, preferred_element_type=jnp.float32
    ).astype(jnp.bfloat16)
    d_value = jnp.einsum(
        "bqk,bqd->bkd", rounded, d_attn, preferred_element_type=jnp.float32
    ).astype(jnp.bfloat16)
    d_pack = jnp.concatenate([d_query, d_key, d_value], axis=2).reshape(group_rows, 3 * HS)
    grad_part = lax.dot_general(
        d_pack, group_shaped, (((0,), (0,)), ((), ())), preferred_element_type=jnp.float32
    )
    grad_part = grad_part.reshape(3 * HS, devices, own_rows).transpose(1, 0, 2)
    grad_qkv = exchange(grad_part.reshape(devices * 3 * HS, own_rows), devices, devices, 3)
    grad_qkv = grad_qkv.reshape(devices // members, local_heads, 3, HS, own_rows)
    grad_qkv = jnp.sum(grad_qkv, axis=0).transpose(3, 1, 0, 2)
    grad_qkv = grad_qkv.reshape(own_rows, 3, local_inner)
    d_proj_blocks = d_proj_mine.reshape(count, devices, own_rows).transpose(1, 0, 2)
    d_proj_own = exchange(
        d_proj_blocks.reshape(devices * count, own_rows), devices, devices, 4
    )
    d_proj_own = join_halves(d_proj_own).reshape(halves, devices, count, own_rows)
    d_proj_own = d_proj_own.transpose(1, 0, 2, 3).reshape(devices * rows_all, own_rows)
    grad_out = lax.dot_general(
        d_proj_own, attended_all, (((0,), (0,)), ((), ())), preferred_element_type=jnp.float32
    )
    squares = jnp.sum(grad_qkv * grad_qkv) + jnp.sum(grad_out * grad_out)
    line = lax.broadcasted_iota(jnp.int32, (8, 128), 0)
    sums = exchange(jnp.where(line == 0, loss_part, squares), devices, 1, 6)
    sums = jnp.sum(sums.reshape(devices, 8, 128), axis=0)
    if halves == 2:
        sums = sums + lax.ppermute(sums, "mp", swap)
    else:
        sums = lax.psum(sums, "mp")
    loss_sum, squares = (sums[0, 0], sums[1, 0])
    rms_value = jnp.sqrt(squares / (4 * D * INNER))
    factor = 1.0 / jnp.maximum(rms_value, 1.0)

    def adam(moment, second, grad):
        normed_grad = grad * factor
        new_moment = BETA_ONE * moment + (1.0 - BETA_ONE) * normed_grad
        new_second = BETA_TWO * second + (1.0 - BETA_TWO) * normed_grad * normed_grad
        return (new_moment, new_second, new_moment / (jnp.sqrt(new_second) + ADAM_EPS))

    mq, vq, uq = adam(moment_qkv, second_qkv, grad_qkv)
    mo, vo, uo = adam(moment_out, second_out, grad_out)
    loss = loss_sum / (samples * lax.axis_size("dp") * LATENT)
    return (mq, vq, uq, mo, vo, uo, loss)


def solution(mesh):
    placed = (
        P("dp", None),
        P("dp", None),
        P("dp"),
        P("dp"),
        P(),
        P(),
        P(),
        P(),
        P(None, None, "mp"),
        P(None, "mp"),
        P(),
        P(),
        P(),
        P("dp", None, "mp"),
        P("dp", "mp"),
        P("dp", None, "mp"),
        P("dp", None, "mp"),
        P("dp", "mp"),
        P("dp", "mp"),
    )
    return jax.shard_map(
        per_device,
        mesh=mesh,
        in_specs=placed,
        out_specs=(
            P("dp", None, "mp"),
            P("dp", None, "mp"),
            P("dp", None, "mp"),
            P("dp", "mp"),
            P("dp", "mp"),
            P("dp", "mp"),
            P(),
        ),
        check_vma=False,
    )
```
